32 devices in a mesh: ctx: 8 (over z, x), head: 4 (over y, core).
Axes of the slice: x: 2, y: 2, z: 4, core: 2. Of those that a mesh axis runs over, the one named last changes fastest.
Arguments:
- tokens: bfloat16 [2048, 4096], P('ctx', 'head'), may hold values from -96 to 96
- w_query: bfloat16 [4096, 2048], P(None, 'head'), may hold values from -0.1875 to 0.1875
- key_matrix: bfloat16 [4096, 512], P(None, 'head'), may hold values from -0.09375 to 0.09375
- value_matrix: bfloat16 [4096, 512], P(None, 'head'), may hold values from -0.09375 to 0.09375
- w_output: bfloat16 [2048, 4096], P('head'), may hold values from -0.125 to 0.125
Outputs:
- mixed: bfloat16 [2048, 4096], P('ctx', 'head')
The draws below stay inside these ranges and needn't reach their ends.
All inputs are finite; a program needn't handle non-finite values.
Results may differ from the reference program's by a relative error of at most 0.013.
The reference program's roundings to bfloat16 on the way (of `query`, `keys`, `values`, `rounded` and `attended`) count: a program that leaves them out, or rounds other values in their place, can miss the bound.
Values may be sent and summed in bfloat16 or wider, within the bound.
A program may use at most 64 MiB of HBM per device.

```python
import jax
import jax.numpy as jnp
from jax import lax

MODEL_WIDTH = 4096
QUERY_HEADS = 16
KEY_VALUE_HEADS = 4
HEAD_SIZE = 128
LENGTH = 2048


def draw_tokens(key, part):
    rows = LENGTH
    base = jnp.clip(jax.random.normal(jax.random.fold_in(key, 1), (rows, MODEL_WIDTH), jnp.float32), -6.0, 6.0)
    return base.astype(jnp.bfloat16)


def steps_of(own_key, shape, shards, low, top_value):
    factor_of = 1.0
    for axis_at, blocks in shards:
        draws = jax.random.uniform(jax.random.fold_in(jax.random.fold_in(own_key, 6), axis_at), (blocks,), jnp.float32, low / len(shards), top_value / len(shards))
        factor_of = factor_of * jnp.repeat(jnp.exp(draws), shape[axis_at] // blocks).reshape((-1,) + (1,) * (len(shape) - 1 - axis_at))
    return factor_of


def noise(own_key, dims, deviation, most, cuts=(), kind=jnp.bfloat16):
    entries = deviation * jax.random.normal(own_key, dims, jnp.float32)
    if cuts:
        entries = entries * steps_of(own_key, dims, cuts, -0.22, 0.18)
    return jnp.clip(entries, -most, most).astype(kind)


def setup_inputs(seed: int = 0) -> dict:
    arg_keys = jax.random.split(jax.random.key(seed), 6)
    tokens = draw_tokens(jax.random.fold_in(arg_keys[5], 71), 0)
    w_query = noise(arg_keys[1], (MODEL_WIDTH, QUERY_HEADS * HEAD_SIZE), (MODEL_WIDTH // 4) ** -0.5, 0.1875, ((1, 4),))
    key_matrix = noise(arg_keys[2], (MODEL_WIDTH, KEY_VALUE_HEADS * HEAD_SIZE), MODEL_WIDTH ** -0.5, 0.09375, ((1, 4),))
    value_matrix = noise(arg_keys[3], (MODEL_WIDTH, KEY_VALUE_HEADS * HEAD_SIZE), MODEL_WIDTH ** -0.5, 0.09375, ((1, 4),))
    w_output = noise(arg_keys[4], (QUERY_HEADS * HEAD_SIZE, MODEL_WIDTH), (QUERY_HEADS * HEAD_SIZE) ** -0.5, 0.125, ((0, 4),))
    return {"tokens": tokens, "w_query": w_query, "key_matrix": key_matrix, "value_matrix": value_matrix, "w_output": w_output}


neg_large = -1.0e30


def reference(tokens, w_query, key_matrix, value_matrix, w_output):
    query = jnp.dot(tokens, w_query, preferred_element_type=jnp.float32).astype(jnp.bfloat16)
    keys = jnp.dot(tokens, key_matrix, preferred_element_type=jnp.float32).astype(jnp.bfloat16)
    values = jnp.dot(tokens, value_matrix, preferred_element_type=jnp.float32).astype(jnp.bfloat16)
    query_group = QUERY_HEADS // KEY_VALUE_HEADS
    scale = HEAD_SIZE ** -0.5
    block = min(512, LENGTH)
    blocks = LENGTH // block
    positions = jnp.arange(LENGTH, dtype=jnp.int32)

    def head_cluster(index):
        key_head = lax.dynamic_slice_in_dim(keys, index * HEAD_SIZE, HEAD_SIZE, 1).astype(jnp.float32)
        value_head = lax.dynamic_slice_in_dim(values, index * HEAD_SIZE, HEAD_SIZE, 1).astype(jnp.float32)
        query_heads = lax.dynamic_slice_in_dim(query, index * query_group * HEAD_SIZE, query_group * HEAD_SIZE, 1).reshape(LENGTH, query_group, HEAD_SIZE)

        def query_block(block_index):
            first = block_index * block
            piece = lax.dynamic_slice_in_dim(query_heads, first, block, 0).astype(jnp.float32)
            scores = jnp.einsum("qgd,td->gqt", piece, key_head) * scale
            query_places = first + jnp.arange(block, dtype=jnp.int32)
            allowed = positions[None, :] <= query_places[:, None]
            top = jnp.max(jnp.where(allowed, scores, neg_large), axis=-1)
            weights = jnp.where(allowed, jnp.exp(scores - top[..., None]), 0.0)
            total = jnp.sum(weights, axis=-1)
            rounded = lax.optimization_barrier(weights.astype(jnp.bfloat16))
            summed = jnp.einsum("gqt,td->gqd", rounded.astype(jnp.float32), value_head)
            return (summed / total[..., None]).astype(jnp.bfloat16)

        output = lax.map(query_block, jnp.arange(blocks, dtype=jnp.int32))
        return output.transpose(0, 2, 1, 3).reshape(LENGTH, query_group * HEAD_SIZE)

    head_list = lax.map(head_cluster, jnp.arange(KEY_VALUE_HEADS, dtype=jnp.int32))
    attended = head_list.transpose(1, 0, 2).reshape(LENGTH, QUERY_HEADS * HEAD_SIZE)
    return jnp.dot(attended, w_output, preferred_element_type=jnp.float32).astype(jnp.bfloat16)
```

```python
import functools
import math

import jax
import jax.numpy as jnp
from jax import lax
from jax.experimental import pallas as pl
from jax.experimental.pallas import tpu as pltpu
from jax.sharding import PartitionSpec as P

MESH = pl.DeviceIdType.MESH
CHUNKS = 4
NEG_LARGE = -1e30


def layer_kernel(
    n_ctx,
    n_head,
    tokens,
    wq_hbm,
    wk_hbm,
    wv_hbm,
    wo_hbm,
    out,
    wq,
    wkv,
    wo,
    gathered,
    kv,
    query,
    scores,
    own_sum,
    across_sum,
    diag_send,
    across_part,
    across_send,
    pair_send,
    pair_part,
    far_part,
    w_sem,
    t_send,
    t_recv,
    kv_direct,
    kv_pair,
    kv_recv,
    r_send,
    r_recv,
):
    rows, depth = tokens.shape
    size = wk_hbm.shape[1]
    group = wq_hbm.shape[1] // size
    chunks = query.shape[0]
    step = rows // chunks
    c = lax.axis_index("ctx")
    h = lax.axis_index("head")
    place, side = c // 2, c % 2
    core = h % 2
    pair = h + 1 - 2 * core
    across = (h + 2) % n_head
    diag = across + 1 - 2 * core
    ctx_pair = c + 1 - 2 * side
    columns = n_ctx // 2

    loads = (
        pltpu.make_async_copy(wq_hbm, wq, w_sem.at[0]),
        pltpu.make_async_copy(wk_hbm, wkv.at[:, pl.ds(0, size)], w_sem.at[1]),
        pltpu.make_async_copy(wv_hbm, wkv.at[:, pl.ds(size, size)], w_sem.at[2]),
        pltpu.make_async_copy(wo_hbm, wo, w_sem.at[3]),
    )
    for load in loads:
        load.start()

    barrier = pltpu.get_barrier_semaphore()
    for other in (pair, across):
        pl.semaphore_signal(barrier, inc=1, device_id={"head": other}, device_id_type=MESH)
    pl.semaphore_signal(barrier, inc=1, device_id={"ctx": ctx_pair}, device_id_type=MESH)
    for shift in range(1, columns):
        other = ((place + shift) % columns) * 2 + side
        pl.semaphore_signal(barrier, inc=1, device_id={"ctx": other}, device_id_type=MESH)
    pl.semaphore_wait(barrier, 2 + columns)

    def part(k):
        return pl.ds(pl.multiple_of(k * step, step), step)

    def token_copy(kind, k):
        src = gathered.at[1, part(k)] if kind == 2 else tokens.at[part(k)]
        return pltpu.make_async_remote_copy(
            src_ref=src,
            dst_ref=gathered.at[kind, part(k)],
            send_sem=t_send.at[kind, k],
            recv_sem=t_recv.at[kind, k],
            device_id={"head": across if kind == 1 else pair},
            device_id_type=MESH,
        )

    def kv_copy(block, k, sem, target):
        return pltpu.make_async_remote_copy(
            src_ref=kv.at[block, part(k)],
            dst_ref=kv.at[block, part(k)],
            send_sem=sem,
            recv_sem=kv_recv.at[block, k],
            device_id={"ctx": target},
            device_id_type=MESH,
        )

    def direct_copy(shift, k):
        return kv_copy(c, k, kv_direct.at[shift, k], c + 2 * shift)

    def pair_copy(where, k):
        return kv_copy(2 * where + side, k, kv_pair.at[where, k], ctx_pair)

    later = columns - 1 - place

    for k in range(chunks):
        token_copy(1, k).start()
        token_copy(0, k).start()

    for load in loads[:3]:
        load.wait()

    def relay(k):
        def one(where, carry):
            pair_copy(where, k).wait_recv()
            pair_copy(where, k).start()
            return carry

        lax.fori_loop(0, place, one, 0)

    def project(k, carry):
        def terms(left, block):
            at = pl.ds(pl.multiple_of(block * depth, depth), depth)
            return (
                jnp.dot(left, wq[at, :], preferred_element_type=jnp.float32),
                jnp.dot(left, wkv[at, :], preferred_element_type=jnp.float32),
            )

        q0, s0 = terms(tokens[part(k), :], h)
        token_copy(0, k).wait_recv()
        q1, s1 = terms(gathered[0, part(k), :], pair)
        q0, s0 = q0 + q1, s0 + s1
        token_copy(1, k).wait_recv()
        token_copy(2, k).start()
        q1, s1 = terms(gathered[1, part(k), :], across)
        q0, s0 = q0 + q1, s0 + s1

        @pl.when(k > 0)
        def _():
            relay(k - 1)

        token_copy(2, k).wait_recv()
        q1, s1 = terms(gathered[2, part(k), :], diag)
        q0, s0 = q0 + q1, s0 + s1
        kv[c, part(k), :] = s0.astype(jnp.bfloat16)
        for g in range(group):
            query[k, pl.ds(g * step, step), :] = q0[:, g * size : (g + 1) * size].astype(
                jnp.bfloat16
            )

        def send(index, carry):
            direct_copy(later - index, k).start()
            return carry

        lax.fori_loop(0, later, send, 0)
        pair_copy(place, k).start()
        return carry

    lax.fori_loop(0, chunks, project, 0)
    relay(chunks - 1)
    loads[3].wait()

    def arrive(index, carry):
        where, k = index // chunks, index % chunks
        kv_copy(2 * where + 1 - side, k, kv_pair.at[where, k], ctx_pair).wait_recv()
        return carry

    lax.fori_loop(0, (place + 1) * chunks, arrive, 0)

    tall = group * step
    wide = 2 * rows
    factor = (size ** (-0.5)) * math.log2(math.e)

    def fold(values, op):
        result = values[:, :size]
        for index in range(1, wide // size):
            result = op(result, values[:, index * size : (index + 1) * size])
        return result

    def reduce_copy(kind, k):
        src = (diag_send, pair_send, across_send)[kind]
        dst = (across_part, pair_part, far_part)[kind]
        return pltpu.make_async_remote_copy(
            src_ref=src.at[k],
            dst_ref=dst.at[k],
            send_sem=r_send.at[kind, k],
            recv_sem=r_recv.at[kind, k],
            device_id={"head": across if kind == 2 else pair},
            device_id_type=MESH,
        )

    def attend(k, carry):
        queries = query[k]

        def score(where):
            keys = kv[pl.ds(2 * where, 2), :, pl.ds(0, size)].reshape(wide, size)
            return lax.dot_general(
                queries, keys, (((1,), (1,)), ((), ())), preferred_element_type=jnp.float32
            )

        at_key = lax.broadcasted_iota(jnp.int32, (step, wide), 1)
        at_query = lax.broadcasted_iota(jnp.int32, (step, wide), 0) + (side * rows + k * step)
        allowed = jnp.concatenate([at_key <= at_query] * group, axis=0)
        last = jnp.where(allowed, score(place), NEG_LARGE)
        scores[place] = last

        def first_pass(where, top):
            found = score(where)
            scores[where] = found
            return jnp.maximum(top, fold(found, jnp.maximum))

        top = lax.fori_loop(0, place, first_pass, fold(last, jnp.maximum))
        top = jnp.max(top, axis=-1, keepdims=True)

        def second_pass(where, state):
            total, summed = state
            weights = jnp.exp2((scores[where] - top) * factor)
            values = kv[pl.ds(2 * where, 2), :, pl.ds(size, size)].reshape(wide, size)
            summed = summed + jnp.dot(
                weights.astype(jnp.bfloat16), values, preferred_element_type=jnp.float32
            )
            return total + fold(weights, jnp.add), summed

        zero = jnp.zeros((tall, size), jnp.float32)
        total, summed = lax.fori_loop(0, place + 1, second_pass, (zero, zero))
        total = jnp.sum(total, axis=-1, keepdims=True)
        heads = (summed / total).astype(jnp.bfloat16)
        attended = jnp.concatenate(
            [heads[g * step : (g + 1) * step] for g in range(group)], axis=1
        )

        def mix(block):
            at = pl.ds(pl.multiple_of(block * depth, depth), depth)
            return jnp.dot(attended, wo[:, at], preferred_element_type=jnp.float32)

        diag_send[k] = mix(diag).astype(jnp.bfloat16)
        reduce_copy(0, k).start()
        across_sum[...] = mix(across)
        pair_send[k] = mix(pair).astype(jnp.bfloat16)
        reduce_copy(1, k).start()
        own_sum[k] = mix(h)
        reduce_copy(0, k).wait_recv()
        across_send[k] = (across_sum[...] + across_part[k].astype(jnp.float32)).astype(
            jnp.bfloat16
        )
        reduce_copy(2, k).start()
        return carry

    lax.fori_loop(0, chunks, attend, 0)

    def finish(k, carry):
        reduce_copy(1, k).wait_recv()
        reduce_copy(2, k).wait_recv()
        out[part(k), :] = (
            own_sum[k] + pair_part[k].astype(jnp.float32) + far_part[k].astype(jnp.float32)
        ).astype(out.dtype)
        return carry

    lax.fori_loop(0, chunks, finish, 0)

    def drain(k, carry):
        for kind in range(3):
            token_copy(kind, k).wait_send()
            reduce_copy(kind, k).wait_send()

        def sent(index, carry):
            direct_copy(later - index, k).wait_send()
            return carry

        lax.fori_loop(0, later, sent, 0)

        def passed(where, carry):
            pair_copy(where, k).wait_send()
            return carry

        lax.fori_loop(0, place + 1, passed, 0)
        return carry

    lax.fori_loop(0, chunks, drain, 0)


def solution(mesh):
    n_ctx, n_head = mesh.shape["ctx"], mesh.shape["head"]

    def local(tokens, w_query, key_matrix, value_matrix, w_output):
        rows, depth = tokens.shape
        width, size = key_matrix.shape
        group = w_query.shape[1] // size
        chunks = CHUNKS
        step = rows // chunks
        bf16, f32 = jnp.bfloat16, jnp.float32
        dma = pltpu.SemaphoreType.DMA
        piece = pltpu.VMEM((chunks, step, depth), bf16)
        anywhere = pl.BlockSpec(memory_space=pl.ANY)
        return pl.pallas_call(
            functools.partial(layer_kernel, n_ctx, n_head),
            out_shape=jax.ShapeDtypeStruct((rows, depth), bf16),
            in_specs=[pl.BlockSpec(memory_space=pltpu.VMEM)] + [anywhere] * 4,
            out_specs=pl.BlockSpec(memory_space=pltpu.VMEM),
            scratch_shapes=[
                pltpu.VMEM(w_query.shape, bf16),
                pltpu.VMEM((width, 2 * size), bf16),
                pltpu.VMEM(w_output.shape, bf16),
                pltpu.VMEM((3, rows, depth), bf16),
                pltpu.VMEM((n_ctx, rows, 2 * size), bf16),
                pltpu.VMEM((chunks, group * step, size), bf16),
                pltpu.VMEM((n_ctx // 2, group * step, 2 * rows), f32),
                pltpu.VMEM((chunks, step, depth), f32),
                pltpu.VMEM((step, depth), f32),
                piece,
                piece,
                piece,
                piece,
                piece,
                piece,
                dma((4,)),
                dma((3, chunks)),
                dma((3, chunks)),
                dma((n_ctx // 2, chunks)),
                dma((n_ctx // 2, chunks)),
                dma((n_ctx, chunks)),
                dma((3, chunks)),
                dma((3, chunks)),
            ],
            compiler_params=pltpu.CompilerParams(
                collective_id=0,
                has_side_effects=True,
                vmem_limit_bytes=60 * 1024 * 1024,
            ),
        )(tokens, w_query, key_matrix, value_matrix, w_output)

    return jax.shard_map(
        local,
        mesh=mesh,
        in_specs=(
            P("ctx", "head"),
            P(None, "head"),
            P(None, "head"),
            P(None, "head"),
            P("head", None),
        ),
        out_specs=P("ctx", "head"),
        check_vma=False,
    )
```

```python
import functools
import math

import jax
import jax.numpy as jnp
from jax import lax
from jax.experimental import pallas as pl
from jax.experimental.pallas import tpu as pltpu
from jax.sharding import PartitionSpec as P

MESH = pl.DeviceIdType.MESH
CHUNKS = 4
PIECES = (4, 4, 4, 4)
UNROLLED = 4
NEG_LARGE = -1e30


def layer_kernel(
    n_ctx,
    n_head,
    tokens,
    wq_hbm,
    wk_hbm,
    wv_hbm,
    wo_hbm,
    out,
    wq,
    wkv,
    wo,
    gathered,
    kv,
    query,
    scores,
    own_sum,
    across_sum,
    diag_send,
    across_part,
    across_send,
    pair_send,
    pair_part,
    far_part,
    mixed_heads,
    w_sem,
    t_send,
    t_recv,
    kv_direct,
    kv_pair,
    kv_recv,
    r_send,
    r_recv,
):
    rows, depth = tokens.shape
    size = wk_hbm.shape[1]
    group = wq_hbm.shape[1] // size
    chunks = own_sum.shape[0]
    step = rows // chunks
    unit = rows // sum(PIECES)
    pieces = len(PIECES)
    lengths = [count * unit for count in PIECES]
    starts = [sum(lengths[:index]) for index in range(pieces)]
    c = lax.axis_index("ctx")
    h = lax.axis_index("head")
    place, side = c // 2, c % 2
    core = h % 2
    pair = h + 1 - 2 * core
    across = (h + 2) % n_head
    diag = across + 1 - 2 * core
    ctx_pair = c + 1 - 2 * side
    columns = n_ctx // 2

    loads = (
        pltpu.make_async_copy(wq_hbm, wq, w_sem.at[0]),
        pltpu.make_async_copy(wk_hbm, wkv.at[:, pl.ds(0, size)], w_sem.at[1]),
        pltpu.make_async_copy(wv_hbm, wkv.at[:, pl.ds(size, size)], w_sem.at[2]),
        pltpu.make_async_copy(wo_hbm, wo, w_sem.at[3]),
    )
    for load in loads:
        load.start()

    barrier = pltpu.get_barrier_semaphore()
    for other in (pair, across):
        pl.semaphore_signal(barrier, inc=1, device_id={"head": other}, device_id_type=MESH)
    pl.semaphore_signal(barrier, inc=1, device_id={"ctx": ctx_pair}, device_id_type=MESH)
    for shift in range(1, columns):
        other = ((place + shift) % columns) * 2 + side
        pl.semaphore_signal(barrier, inc=1, device_id={"ctx": other}, device_id_type=MESH)
    pl.semaphore_wait(barrier, 2 + columns)

    def part(k):
        return pl.ds(pl.multiple_of(k * step, step), step)

    def piece(k):
        return pl.ds(starts[k], lengths[k])

    def token_copy(kind, k):
        src = gathered.at[1, piece(k)] if kind == 2 else tokens.at[piece(k)]
        return pltpu.make_async_remote_copy(
            src_ref=src,
            dst_ref=gathered.at[kind, piece(k)],
            send_sem=t_send.at[kind, k],
            recv_sem=t_recv.at[kind, k],
            device_id={"head": across if kind == 1 else pair},
            device_id_type=MESH,
        )

    def kv_copy(block, k, sem, target):
        return pltpu.make_async_remote_copy(
            src_ref=kv.at[block, piece(k)],
            dst_ref=kv.at[block, piece(k)],
            send_sem=sem,
            recv_sem=kv_recv.at[block, k],
            device_id={"ctx": target},
            device_id_type=MESH,
        )

    def direct_copy(shift, k):
        return kv_copy(c, k, kv_direct.at[shift, k], c + 2 * shift)

    def pair_copy(where, k):
        return kv_copy(2 * where + side, k, kv_pair.at[where, k], ctx_pair)

    later = columns - 1 - place

    for k in range(pieces):
        token_copy(1, k).start()
        token_copy(0, k).start()

    for load in loads[:3]:
        load.wait()

    def relay(k):
        def one(where, carry):
            pair_copy(where, k).wait_recv()
            pair_copy(where, k).start()
            return carry

        lax.fori_loop(0, place, one, 0)

    def project(k):
        def rows_of(block):
            return pl.ds(pl.multiple_of(block * depth, depth), depth)

        def q_term(left, block):
            return jnp.dot(left, wq[rows_of(block), :], preferred_element_type=jnp.float32)

        def s_term(left, block):
            return jnp.dot(left, wkv[rows_of(block), :], preferred_element_type=jnp.float32)

        left = tokens[piece(k), :]
        both, q_sum = s_term(left, h), q_term(left, h)
        token_copy(0, k).wait_recv()
        left = gathered[0, piece(k), :]
        both, q_sum = both + s_term(left, pair), q_sum + q_term(left, pair)
        token_copy(1, k).wait_recv()
        token_copy(2, k).start()
        left = gathered[1, piece(k), :]
        both, q_sum = both + s_term(left, across), q_sum + q_term(left, across)
        if k > 0:
            relay(k - 1)
        token_copy(2, k).wait_recv()
        left = gathered[2, piece(k), :]
        kv[c, piece(k), :] = (both + s_term(left, diag)).astype(jnp.bfloat16)

        def send(index, carry):
            direct_copy(later - index, k).start()
            return carry

        lax.fori_loop(0, later, send, 0)
        pair_copy(place, k).start()
        q_sum = q_sum + q_term(left, diag)
        for g in range(group):
            query[g, piece(k), :] = q_sum[:, g * size : (g + 1) * size].astype(jnp.bfloat16)

    for k in range(pieces):
        project(k)
    relay(pieces - 1)
    loads[3].wait()

    def arrive(where, carry):
        for k in range(pieces):
            kv_copy(2 * where + 1 - side, k, kv_pair.at[where, k], ctx_pair).wait_recv()
        return carry

    lax.fori_loop(0, place + 1, arrive, 0)

    tall = group * step
    wide = 2 * rows
    factor = (size ** (-0.5)) * math.log2(math.e)

    def fold(values, op):
        result = values[:, :size]
        for index in range(1, wide // size):
            result = op(result, values[:, index * size : (index + 1) * size])
        return result

    def reduce_copy(kind, k):
        src = (diag_send, pair_send, across_send)[kind]
        dst = (across_part, pair_part, far_part)[kind]
        return pltpu.make_async_remote_copy(
            src_ref=src.at[k],
            dst_ref=dst.at[k],
            send_sem=r_send.at[kind, k],
            recv_sem=r_recv.at[kind, k],
            device_id={"head": across if kind == 2 else pair},
            device_id_type=MESH,
        )

    def attention(k, count):
        queries = query[:, part(k), :].reshape(tall, size)

        def score(where):
            keys = kv[pl.ds(2 * where, 2), :, pl.ds(0, size)].reshape(wide, size)
            return lax.dot_general(
                queries, keys, (((1,), (1,)), ((), ())), preferred_element_type=jnp.float32
            )

        at_key = lax.broadcasted_iota(jnp.int32, (step, wide), 1)
        at_query = lax.broadcasted_iota(jnp.int32, (step, wide), 0) + (side * rows + k * step)
        allowed = jnp.concatenate([at_key <= at_query] * group, axis=0)
        last = jnp.where(allowed, score(count), NEG_LARGE)
        scores[count] = last

        def first_pass(where, top):
            found = score(where)
            scores[where] = found
            return jnp.maximum(top, fold(found, jnp.maximum))

        def second_pass(where, state):
            total, summed = state
            weights = jnp.exp2((scores[where] - top) * factor)
            values = kv[pl.ds(2 * where, 2), :, pl.ds(size, size)].reshape(wide, size)
            summed = summed + jnp.dot(
                weights.astype(jnp.bfloat16), values, preferred_element_type=jnp.float32
            )
            return total + fold(weights, jnp.add), summed

        top = fold(last, jnp.maximum)
        state = (jnp.zeros((tall, size), jnp.float32),) * 2
        if isinstance(count, int):
            for where in range(count):
                top = first_pass(where, top)
            top = jnp.max(top, axis=-1, keepdims=True)
            for where in range(count + 1):
                state = second_pass(where, state)
        else:
            top = lax.fori_loop(0, count, first_pass, top)
            top = jnp.max(top, axis=-1, keepdims=True)
            state = lax.fori_loop(0, count + 1, second_pass, state)
        total, summed = state
        total = jnp.sum(total, axis=-1, keepdims=True)
        heads = (summed / total).astype(jnp.bfloat16)
        for g in range(group):
            mixed_heads[:, pl.ds(g * size, size)] = heads[g * step : (g + 1) * step]

    def attend(k, carry):
        if columns <= UNROLLED:
            for count in range(columns):
                pl.when(place == count)(functools.partial(attention, k, count))
        else:
            attention(k, place)
        attended = mixed_heads[...]

        def mix(block):
            at = pl.ds(pl.multiple_of(block * depth, depth), depth)
            return jnp.dot(attended, wo[:, at], preferred_element_type=jnp.float32)

        diag_send[k] = mix(diag).astype(jnp.bfloat16)
        reduce_copy(0, k).start()
        across_sum[...] = mix(across)
        pair_send[k] = mix(pair).astype(jnp.bfloat16)
        reduce_copy(1, k).start()
        own_sum[k] = mix(h)
        reduce_copy(0, k).wait_recv()
        across_send[k] = (across_sum[...] + across_part[k].astype(jnp.float32)).astype(
            jnp.bfloat16
        )
        reduce_copy(2, k).start()
        return carry

    lax.fori_loop(0, chunks, attend, 0)

    def finish(k, carry):
        reduce_copy(1, k).wait_recv()
        reduce_copy(2, k).wait_recv()
        out[part(k), :] = (
            own_sum[k] + pair_part[k].astype(jnp.float32) + far_part[k].astype(jnp.float32)
        ).astype(out.dtype)
        return carry

    lax.fori_loop(0, chunks, finish, 0)

    for kind in range(3):
        for k in range(pieces):
            token_copy(kind, k).wait_send()
        for k in range(chunks):
            reduce_copy(kind, k).wait_send()

    def sent(index, carry):
        for k in range(pieces):
            direct_copy(later - index, k).wait_send()
        return carry

    lax.fori_loop(0, later, sent, 0)

    def passed(where, carry):
        for k in range(pieces):
            pair_copy(where, k).wait_send()
        return carry

    lax.fori_loop(0, place + 1, passed, 0)


def solution(mesh):
    n_ctx, n_head = mesh.shape["ctx"], mesh.shape["head"]

    def local(tokens, w_query, key_matrix, value_matrix, w_output):
        rows, depth = tokens.shape
        width, size = key_matrix.shape
        group = w_query.shape[1] // size
        chunks = CHUNKS
        step = rows // chunks
        bf16, f32 = jnp.bfloat16, jnp.float32
        dma = pltpu.SemaphoreType.DMA
        piece = pltpu.VMEM((chunks, step, depth), bf16)
        anywhere = pl.BlockSpec(memory_space=pl.ANY)
        return pl.pallas_call(
            functools.partial(layer_kernel, n_ctx, n_head),
            out_shape=jax.ShapeDtypeStruct((rows, depth), bf16),
            in_specs=[pl.BlockSpec(memory_space=pltpu.VMEM)] + [anywhere] * 4,
            out_specs=pl.BlockSpec(memory_space=pltpu.VMEM),
            scratch_shapes=[
                pltpu.VMEM(w_query.shape, bf16),
                pltpu.VMEM((width, 2 * size), bf16),
                pltpu.VMEM(w_output.shape, bf16),
                pltpu.VMEM((3, rows, depth), bf16),
                pltpu.VMEM((n_ctx, rows, 2 * size), bf16),
                pltpu.VMEM((group, rows, size), bf16),
                pltpu.VMEM((n_ctx // 2, group * step, 2 * rows), f32),
                pltpu.VMEM((chunks, step, depth), f32),
                pltpu.VMEM((step, depth), f32),
                piece,
                piece,
                piece,
                piece,
                piece,
                piece,
                pltpu.VMEM((step, group * size), bf16),
                dma((4,)),
                dma((3, len(PIECES))),
                dma((3, len(PIECES))),
                dma((n_ctx // 2, len(PIECES))),
                dma((n_ctx // 2, len(PIECES))),
                dma((n_ctx, len(PIECES))),
                dma((3, chunks)),
                dma((3, chunks)),
            ],
            compiler_params=pltpu.CompilerParams(
                collective_id=0,
                has_side_effects=True,
                vmem_limit_bytes=60 * 1024 * 1024,
            ),
        )(tokens, w_query, key_matrix, value_matrix, w_output)

    return jax.shard_map(
        local,
        mesh=mesh,
        in_specs=(
            P("ctx", "head"),
            P(None, "head"),
            P(None, "head"),
            P(None, "head"),
            P("head", None),
        ),
        out_specs=P("ctx", "head"),
        check_vma=False,
    )
```

```python
import functools
import math

import jax
import jax.numpy as jnp
from jax import lax
from jax.experimental import pallas as pl
from jax.experimental.pallas import tpu as pltpu
from jax.sharding import PartitionSpec as P

MESH = pl.DeviceIdType.MESH
CHUNKS = 4
PIECES = (4, 4, 4, 4)
UNROLLED = 4
NEG_LARGE = -1e30


def layer_kernel(
    n_ctx,
    n_head,
    tokens,
    wq_hbm,
    wk_hbm,
    wv_hbm,
    wo_hbm,
    out,
    wq,
    wkv,
    wo,
    gathered,
    kv,
    query,
    scores,
    own_sum,
    across_sum,
    diag_send,
    across_part,
    across_send,
    pair_send,
    pair_part,
    far_part,
    mixed_heads,
    w_sem,
    t_send,
    t_recv,
    kv_direct,
    kv_pair,
    kv_recv,
    r_send,
    r_recv,
):
    rows, depth = tokens.shape
    size = wk_hbm.shape[1]
    group = wq_hbm.shape[1] // size
    chunks = own_sum.shape[0]
    step = rows // chunks
    unit = rows // sum(PIECES)
    pieces = len(PIECES)
    lengths = [count * unit for count in PIECES]
    starts = [sum(lengths[:index]) for index in range(pieces)]
    c = lax.axis_index("ctx")
    h = lax.axis_index("head")
    place, side = c // 2, c % 2
    core = h % 2
    pair = h + 1 - 2 * core
    across = (h + 2) % n_head
    diag = across + 1 - 2 * core
    ctx_pair = c + 1 - 2 * side
    columns = n_ctx // 2

    barrier = pltpu.get_barrier_semaphore()
    for shift in range(1, columns):
        other = ((place + shift) % columns) * 2 + side
        pl.semaphore_signal(barrier, inc=1, device_id={"ctx": other}, device_id_type=MESH)
    pl.semaphore_signal(barrier, inc=1, device_id={"ctx": ctx_pair}, device_id_type=MESH)
    for other in (pair, across):
        pl.semaphore_signal(barrier, inc=1, device_id={"head": other}, device_id_type=MESH)
    loads = (
        pltpu.make_async_copy(wq_hbm, wq, w_sem.at[0]),
        pltpu.make_async_copy(wk_hbm, wkv.at[:, pl.ds(0, size)], w_sem.at[1]),
        pltpu.make_async_copy(wv_hbm, wkv.at[:, pl.ds(size, size)], w_sem.at[2]),
        pltpu.make_async_copy(wo_hbm, wo, w_sem.at[3]),
    )
    for load in loads:
        load.start()
    pl.semaphore_wait(barrier, 2 + columns)

    def part(k):
        return pl.ds(pl.multiple_of(k * step, step), step)

    def piece(k):
        return pl.ds(starts[k], lengths[k])

    def token_copy(kind, k):
        src = gathered.at[1, piece(k)] if kind == 2 else tokens.at[piece(k)]
        return pltpu.make_async_remote_copy(
            src_ref=src,
            dst_ref=gathered.at[kind, piece(k)],
            send_sem=t_send.at[kind, k],
            recv_sem=t_recv.at[kind, k],
            device_id={"head": across if kind == 1 else pair},
            device_id_type=MESH,
        )

    def kv_copy(block, k, sem, target):
        return pltpu.make_async_remote_copy(
            src_ref=kv.at[block, piece(k)],
            dst_ref=kv.at[block, piece(k)],
            send_sem=sem,
            recv_sem=kv_recv.at[block, k],
            device_id={"ctx": target},
            device_id_type=MESH,
        )

    def direct_copy(shift, k):
        return kv_copy(c, k, kv_direct.at[shift, k], c + 2 * shift)

    def pair_copy(where, k):
        return kv_copy(2 * where + side, k, kv_pair.at[where, k], ctx_pair)

    later = columns - 1 - place

    for k in range(pieces):
        token_copy(1, k).start()
        token_copy(0, k).start()

    for load in loads[:3]:
        load.wait()

    def relay(k):
        def one(where, carry):
            pair_copy(where, k).wait_recv()
            pair_copy(where, k).start()
            return carry

        lax.fori_loop(0, place, one, 0)

    def project(k):
        def rows_of(block):
            return pl.ds(pl.multiple_of(block * depth, depth), depth)

        def q_term(left, block):
            return jnp.dot(left, wq[rows_of(block), :], preferred_element_type=jnp.float32)

        def s_term(left, block):
            return jnp.dot(left, wkv[rows_of(block), :], preferred_element_type=jnp.float32)

        left = tokens[piece(k), :]
        both, q_sum = s_term(left, h), q_term(left, h)
        token_copy(0, k).wait_recv()
        left = gathered[0, piece(k), :]
        both, q_sum = both + s_term(left, pair), q_sum + q_term(left, pair)
        token_copy(1, k).wait_recv()
        token_copy(2, k).start()
        left = gathered[1, piece(k), :]
        both, q_sum = both + s_term(left, across), q_sum + q_term(left, across)
        token_copy(2, k).wait_recv()
        left = gathered[2, piece(k), :]
        kv[c, piece(k), :] = (both + s_term(left, diag)).astype(jnp.bfloat16)

        def send(index, carry):
            direct_copy(later - index, k).start()
            return carry

        lax.fori_loop(0, later, send, 0)
        pair_copy(place, k).start()
        if k > 0:
            relay(k - 1)
        q_sum = q_sum + q_term(left, diag)
        for g in range(group):
            query[g, piece(k), :] = q_sum[:, g * size : (g + 1) * size].astype(jnp.bfloat16)

    for k in range(pieces):
        project(k)
    relay(pieces - 1)
    loads[3].wait()

    def arrive(where, carry):
        for k in range(pieces):
            kv_copy(2 * where + 1 - side, k, kv_pair.at[where, k], ctx_pair).wait_recv()
        return carry

    lax.fori_loop(0, place + 1, arrive, 0)

    tall = group * step
    wide = 2 * rows
    factor = (size ** (-0.5)) * math.log2(math.e)

    def fold(values, op):
        result = values[:, :size]
        for index in range(1, wide // size):
            result = op(result, values[:, index * size : (index + 1) * size])
        return result

    def reduce_copy(kind, k):
        src = (diag_send, pair_send, across_send)[kind]
        dst = (across_part, pair_part, far_part)[kind]
        return pltpu.make_async_remote_copy(
            src_ref=src.at[k],
            dst_ref=dst.at[k],
            send_sem=r_send.at[kind, k],
            recv_sem=r_recv.at[kind, k],
            device_id={"head": across if kind == 2 else pair},
            device_id_type=MESH,
        )

    def attention(k, count):
        queries = query[:, part(k), :].reshape(tall, size)

        def score(where):
            keys = kv[pl.ds(2 * where, 2), :, pl.ds(0, size)].reshape(wide, size)
            return lax.dot_general(
                queries, keys, (((1,), (1,)), ((), ())), preferred_element_type=jnp.float32
            )

        at_key = lax.broadcasted_iota(jnp.int32, (step, wide), 1)
        at_query = lax.broadcasted_iota(jnp.int32, (step, wide), 0) + (side * rows + k * step)
        allowed = jnp.concatenate([at_key <= at_query] * group, axis=0)
        last = jnp.where(allowed, score(count), NEG_LARGE)
        scores[count] = last

        def first_pass(where, top):
            found = score(where)
            scores[where] = found
            return jnp.maximum(top, fold(found, jnp.maximum))

        def second_pass(where, state):
            total, summed = state
            weights = jnp.exp2((scores[where] - top) * factor)
            values = kv[pl.ds(2 * where, 2), :, pl.ds(size, size)].reshape(wide, size)
            summed = summed + jnp.dot(
                weights.astype(jnp.bfloat16), values, preferred_element_type=jnp.float32
            )
            return total + fold(weights, jnp.add), summed

        top = fold(last, jnp.maximum)
        state = (jnp.zeros((tall, size), jnp.float32),) * 2
        if isinstance(count, int):
            for where in range(count):
                top = first_pass(where, top)
            top = jnp.max(top, axis=-1, keepdims=True)
            for where in range(count + 1):
                state = second_pass(where, state)
        else:
            top = lax.fori_loop(0, count, first_pass, top)
            top = jnp.max(top, axis=-1, keepdims=True)
            state = lax.fori_loop(0, count + 1, second_pass, state)
        total, summed = state
        total = jnp.sum(total, axis=-1, keepdims=True)
        heads = (summed / total).astype(jnp.bfloat16)
        for g in range(group):
            mixed_heads[:, pl.ds(g * size, size)] = heads[g * step : (g + 1) * step]

    def attend(k, carry):
        if columns <= UNROLLED:
            for count in range(columns):
                pl.when(place == count)(functools.partial(attention, k, count))
        else:
            attention(k, place)
        attended = mixed_heads[...]

        def mix(block):
            at = pl.ds(pl.multiple_of(block * depth, depth), depth)
            return jnp.dot(attended, wo[:, at], preferred_element_type=jnp.float32)

        diag_send[k] = mix(diag).astype(jnp.bfloat16)
        reduce_copy(0, k).start()
        across_sum[...] = mix(across)
        own_sum[k] = mix(h)
        reduce_copy(0, k).wait_recv()
        across_send[k] = (across_sum[...] + across_part[k].astype(jnp.float32)).astype(
            jnp.bfloat16
        )
        reduce_copy(2, k).start()
        pair_send[k] = mix(pair).astype(jnp.bfloat16)
        reduce_copy(1, k).start()
        return carry

    lax.fori_loop(0, chunks, attend, 0)

    def finish(k, carry):
        reduce_copy(1, k).wait_recv()
        reduce_copy(2, k).wait_recv()
        out[part(k), :] = (
            own_sum[k] + pair_part[k].astype(jnp.float32) + far_part[k].astype(jnp.float32)
        ).astype(out.dtype)
        return carry

    lax.fori_loop(0, chunks, finish, 0)

    for kind in range(3):
        for k in range(pieces):
            token_copy(kind, k).wait_send()
        for k in range(chunks):
            reduce_copy(kind, k).wait_send()

    def sent(index, carry):
        for k in range(pieces):
            direct_copy(later - index, k).wait_send()
        return carry

    lax.fori_loop(0, later, sent, 0)

    def passed(where, carry):
        for k in range(pieces):
            pair_copy(where, k).wait_send()
        return carry

    lax.fori_loop(0, place + 1, passed, 0)


def solution(mesh):
    n_ctx, n_head = mesh.shape["ctx"], mesh.shape["head"]

    def local(tokens, w_query, key_matrix, value_matrix, w_output):
        rows, depth = tokens.shape
        width, size = key_matrix.shape
        group = w_query.shape[1] // size
        chunks = CHUNKS
        step = rows // chunks
        bf16, f32 = jnp.bfloat16, jnp.float32
        dma = pltpu.SemaphoreType.DMA
        piece = pltpu.VMEM((chunks, step, depth), bf16)
        anywhere = pl.BlockSpec(memory_space=pl.ANY)
        return pl.pallas_call(
            functools.partial(layer_kernel, n_ctx, n_head),
            out_shape=jax.ShapeDtypeStruct((rows, depth), bf16),
            in_specs=[pl.BlockSpec(memory_space=pltpu.VMEM)] + [anywhere] * 4,
            out_specs=pl.BlockSpec(memory_space=pltpu.VMEM),
            scratch_shapes=[
                pltpu.VMEM(w_query.shape, bf16),
                pltpu.VMEM((width, 2 * size), bf16),
                pltpu.VMEM(w_output.shape, bf16),
                pltpu.VMEM((3, rows, depth), bf16),
                pltpu.VMEM((n_ctx, rows, 2 * size), bf16),
                pltpu.VMEM((group, rows, size), bf16),
                pltpu.VMEM((n_ctx // 2, group * step, 2 * rows), f32),
                pltpu.VMEM((chunks, step, depth), f32),
                pltpu.VMEM((step, depth), f32),
                piece,
                piece,
                piece,
                piece,
                piece,
                piece,
                pltpu.VMEM((step, group * size), bf16),
                dma((4,)),
                dma((3, len(PIECES))),
                dma((3, len(PIECES))),
                dma((n_ctx // 2, len(PIECES))),
                dma((n_ctx // 2, len(PIECES))),
                dma((n_ctx, len(PIECES))),
                dma((3, chunks)),
                dma((3, chunks)),
            ],
            compiler_params=pltpu.CompilerParams(
                collective_id=0,
                has_side_effects=True,
                vmem_limit_bytes=60 * 1024 * 1024,
            ),
        )(tokens, w_query, key_matrix, value_matrix, w_output)

    return jax.shard_map(
        local,
        mesh=mesh,
        in_specs=(
            P("ctx", "head"),
            P(None, "head"),
            P(None, "head"),
            P(None, "head"),
            P("head", None),
        ),
        out_specs=P("ctx", "head"),
        check_vma=False,
    )
```
